512 devices in a mesh: rx: 64 (over y_lo, z, core), shot: 8 (over y_hi, x).
Axes of the slice: x: 4, y: 8 (y_hi: 2, y_lo: 4; y = y_hi * 4 + y_lo), z: 8, core: 2. Of those that a mesh axis runs over, the one named last changes fastest.
Arguments:
- data: bfloat16 [3, 2, 4, 128, 512, 128], P(None, None, None, 'rx', 'shot'), may hold values from -6 to 6
- mixing: float32 [3, 2, 4, 4, 128, 128], P(None, None, None, None, 'rx'), may hold values from -3 to 3
- counts: int32 [3, 128], P(None, 'rx'), may hold values from 0 to 64
Outputs:
- fields: bfloat16 [3, 2, 4, 128, 512, 128], P(None, None, None, 'rx', 'shot')
- gram: float32 [3, 2, 128, 128, 128], P(None, None, 'rx', 'shot')
The draws below stay inside these ranges and needn't reach their ends.
All inputs are finite; a program needn't handle non-finite values.
Results may differ from the reference program's by a relative error of at most 0.0091.
Values may be sent and summed in bfloat16 or wider, within the bound.
No kernel may reach another device: no remote copies, remote signals or barrier semaphores. Data moves between devices by JAX's collectives and lax.ppermute only.
A program may use at most 64 MiB of HBM per device.

```python
import math
import jax
import jax.numpy as jnp
from jax import lax

RX = 128
RY = 128
NF = 3
SHOTS_DEV = 64
SHOTS = 512


def set_ends(values, key, low, largest):
    longest = values.shape.index(max(values.shape))
    spots = []
    for shift in (0, 1):
        where = [jax.random.randint(jax.random.fold_in(key, axis), (), 0, length) for axis, length in enumerate(values.shape)]
        where[longest] = (where[longest] + shift) % values.shape[longest]
        spots.append(tuple(where))
    return values.at[spots[0]].set(low).at[spots[1]].set(largest)


def levels(stream_key, extent, pieces, least, high):
    gain, own = 1.0, jax.random.fold_in(stream_key, 6)
    for axis_at, parts in pieces:
        heights = jnp.exp(jax.random.uniform(jax.random.fold_in(own, axis_at), (parts,), jnp.float32, least / len(pieces), high / len(pieces)))
        gain = gain * jnp.repeat(heights, extent[axis_at] // parts).reshape([-1 if axis == axis_at else 1 for axis in range(len(extent))])
    return gain


def noise(own_key, extent, spread, bound, pieces=(), kind=jnp.bfloat16):
    values = jax.random.normal(own_key, extent, jnp.float32) * spread
    if len(pieces) > 0:
        values = levels(own_key, extent, pieces, -0.22, 0.18) * values
    return jnp.clip(values, min=-bound, max=bound).astype(kind)


def setup_inputs(seed: int = 0) -> dict:
    seeds = jax.random.split(jax.random.key(seed), 4)
    data = noise(seeds[0], (NF, 2, 4, RX, SHOTS, RY), 1.0, 6.0, ((3, 64), (4, 8)))
    mixing = noise(seeds[1], (NF, 2, 4, 4, RY, RX), 0.5, 3.0, ((4, 64),), jnp.float32)
    counts = set_ends(jax.random.randint(seeds[2], (NF, RY), 0, RX // 2 + 1), jax.random.fold_in(seeds[2], 1), 0, (RX // 2 + 1) - 1).astype(jnp.int32)
    return dict(data=data, mixing=mixing, counts=counts)


def dft_table(size, sign):
    steps = jnp.arange(size, dtype=jnp.int32)
    phases = steps[:, None] * steps[None, :] % size
    angles = phases.astype(jnp.float32) * (2.0 * math.pi / size)
    factor = 1.0 / math.sqrt(size)
    cosine = jnp.cos(angles) * factor
    sine = jnp.sin(angles) * (factor * sign)
    top_rows = jnp.stack([cosine, -sine], axis=1)
    low_rows = jnp.stack([sine, cosine], axis=1)
    return jnp.stack([top_rows, low_rows], axis=0).astype(jnp.bfloat16)

def apply_mix(matrix, values):
    return jnp.einsum('oikq,ikqs->okqs', matrix, values, precision=lax.Precision.HIGHEST)

def reference(data, mixing, counts):
    ry_forward = dft_table(RY, 1.0).astype(jnp.float32)
    rx_forward = dft_table(RX, 1.0).astype(jnp.float32)
    rx_inverse = dft_table(RX, -1.0).astype(jnp.float32)
    ry_inverse = dft_table(RY, -1.0).astype(jnp.float32)
    wave_index = jnp.arange(RX, dtype=jnp.int32)
    radial = jnp.minimum(wave_index, RX - wave_index)

    def one_bin(item):
        bin_data, bin_mix, bin_counts = item
        passing = (radial[None, :] <= bin_counts[:, None]).astype(jnp.float32)
        blocks = jnp.moveaxis(bin_data.reshape(2, 4, RX, SHOTS // SHOTS_DEV, SHOTS_DEV, RY), 3, 0)

        def one_block(total, block):
            spectra = jnp.einsum('cmxsy,cydk->dmkxs', block.astype(jnp.float32), ry_forward).astype(jnp.bfloat16)
            kspace = jnp.einsum('cmkxs,cxdq->dmkqs', spectra.astype(jnp.float32), rx_forward)
            mixed_real = apply_mix(bin_mix[0], kspace[0]) - apply_mix(bin_mix[1], kspace[1])
            mixed_imag = apply_mix(bin_mix[0], kspace[1]) + apply_mix(bin_mix[1], kspace[0])
            mixed = (jnp.stack([mixed_real, mixed_imag], axis=0) * passing[None, None, :, :, None]).astype(jnp.bfloat16)
            spaced = jnp.einsum('cmkqs,cqdx->dmkxs', mixed.astype(jnp.float32), rx_inverse).astype(jnp.bfloat16)
            downgo = spaced[:, 1].astype(jnp.float32)
            product = jnp.einsum('ckxs,dkzs->cdkxz', downgo, downgo)
            term = jnp.stack([product[0, 0] + product[1, 1], product[1, 0] - product[0, 1]], axis=0)
            fields = jnp.einsum('cmkxs,ckdy->dmxsy', spaced.astype(jnp.float32), ry_inverse).astype(jnp.bfloat16)
            return (total + term, fields)
        total, fields = lax.scan(one_block, jnp.zeros((2, RY, RX, RX), jnp.float32), blocks)
        fields = jnp.moveaxis(fields, 0, 3).reshape(2, 4, RX, SHOTS, RY)
        return (fields, total / SHOTS)
    fields, gram = lax.map(one_bin, (data, mixing, counts))
    return (fields, gram)
```

```python
import functools
import math

import jax
import jax.numpy as jnp
import ml_dtypes
import numpy as np
from jax import lax
from jax.experimental import pallas as pl
from jax.experimental.pallas import tpu as pltpu
from jax.sharding import PartitionSpec as P

BF16 = jnp.bfloat16
F32 = jnp.float32
NT = (((1,), (1,)), ((), ()))
NN = (((1,), (0,)), ((), ()))
SX = 4


def dft_table(size, sign):
    steps = np.arange(size, dtype=np.int64)
    angles = (steps[:, None] * steps[None, :] % size).astype(np.float64) * (2.0 * math.pi / size)
    cosine = np.cos(angles) / math.sqrt(size)
    sine = np.sin(angles) * (sign / math.sqrt(size))
    return np.stack(
        [np.stack([cosine, -sine], axis=1), np.stack([sine, cosine], axis=1)], axis=0
    )


def bf16_const(array):
    return np.ascontiguousarray(array).astype(np.float32).astype(ml_dtypes.bfloat16)


def out_rows(table, per):
    n = table.shape[1]
    t = table.reshape(2, n, 2, n // per, per)
    return bf16_const(t.transpose(2, 4, 3, 0, 1).reshape(2 * n, 2 * n))


def in_rows(table, per):
    n = table.shape[1]
    t = table.reshape(2, n // per, per, 2, n)
    return bf16_const(t.transpose(2, 0, 1, 3, 4).reshape(2 * n, 2 * n))


def dot(a, b, dims):
    return lax.dot_general(a, b, dims, preferred_element_type=F32)


def forward_kernel(devices, data_ref, table_ref, out_ref, rows_ref):
    comps = data_ref.shape[2]
    per = rows_ref.shape[0] // devices
    lines = data_ref.shape[3] * data_ref.shape[4]
    size = data_ref.shape[5]
    table = table_ref[...]
    for m in range(comps):
        both = jnp.concatenate(
            [data_ref[0, c, m].reshape(lines, size) for c in range(2)], axis=1
        )
        res = dot(table, both, NT)
        for d in range(2):
            for p in range(2):
                start = (d * 2 + p) * devices
                rows_ref[pl.ds((d * comps + m) * 2 + p, devices, stride=per), :] = res[
                    start : start + devices
                ]
    out_ref[...] = rows_ref[...].reshape(out_ref.shape).astype(BF16)


def gathered(rows_ref, devices, comps, m):
    per = rows_ref.shape[0] // devices
    halves = []
    for p in range(2):
        both = jnp.concatenate(
            [rows_ref[pl.ds((c * comps + m) * 2 + p, devices, stride=per), :] for c in range(2)],
            axis=0,
        )
        turned = both.T.astype(BF16)
        half = turned.shape[0] // 2
        halves.append(jnp.concatenate([turned[:half], turned[half:]], axis=1))
    return jnp.concatenate(halves, axis=0)


def middle_kernel(
    devices, counts_ref, in_ref, mixing_ref, fwd_ref, inv_ref, out_ref, down_ref, rows_ref, k_ref
):
    f = pl.program_id(0)
    comps = mixing_ref.shape[2]
    size = mixing_ref.shape[5]
    per = rows_ref.shape[0] // devices
    rows_ref[...] = in_ref[...].astype(F32).reshape(rows_ref.shape)
    fwd = fwd_ref[...]
    for m in range(comps):
        k_ref[m] = dot(gathered(rows_ref, devices, comps, m), fwd, NN)
    shots = k_ref.shape[1] // 2
    wave = lax.broadcasted_iota(jnp.int32, (1, size), 1)
    radial = jnp.minimum(wave, size - wave)
    inv = inv_ref[...]
    for o in range(comps):
        parts = []
        for p in range(2):
            passing = (radial <= counts_ref[f, p]).astype(F32)
            span = pl.ds(p * shots, shots)
            real = imag = None
            for i in range(comps):
                a = mixing_ref[0, 0, o, i, p : p + 1, :] * passing
                b = mixing_ref[0, 1, o, i, p : p + 1, :] * passing
                kr = k_ref[i, span, 0:size]
                ki = k_ref[i, span, size : 2 * size]
                r = a * kr - b * ki
                s = a * ki + b * kr
                real = r if real is None else real + r
                imag = s if imag is None else imag + s
            parts.append(jnp.concatenate([real, imag], axis=1).astype(BF16))
        mixed = jnp.concatenate(parts, axis=0)
        if o == 1:
            down_ref[0] = mixed
        res = dot(inv, mixed, NT)
        for d in range(2):
            for l in range(2):
                start = (d * 2 + l) * devices
                rows_ref[pl.ds((d * comps + o) * 2 + l, devices, stride=per), :] = res[
                    start : start + devices
                ]
    out_ref[...] = rows_ref[...].reshape(out_ref.shape).astype(BF16)


def gram_kernel(weight, where_ref, down_ref, inv_ref, own_ref, *rest):
    sent, gram_ref = rest[:-1], rest[-1]
    bins = down_ref.shape[0]
    size = down_ref.shape[2] // 2
    slices = own_ref.shape[0] * (1 + len(sent))
    share = size // slices
    inv = inv_ref[...]
    lane = lax.broadcasted_iota(jnp.int32, (1, down_ref.shape[1]), 1)
    shots = down_ref.shape[1] // 2
    for f in range(bins):
        spaced = dot(inv, down_ref[f], NT).astype(BF16)
        real, imag = spaced[:size], spaced[size:]
        zero = jnp.zeros_like(real)
        left = jnp.concatenate([real, imag], axis=1)
        right = jnp.concatenate(
            [left, jnp.concatenate([-imag, real], axis=1)], axis=0
        )
        for p in range(2):
            keep = (lane >= p * shots) & (lane < (p + 1) * shots)
            part = jnp.concatenate(
                [jnp.where(keep, real, zero), jnp.where(keep, imag, zero)], axis=1
            )
            prod = dot(part, right, NT) * weight
            for c in range(2):
                gram_ref[(f * 2 + c) * 2 + p] = prod[:, c * size : (c + 1) * size]
    here_x, here_y = where_ref[0], where_ref[1]
    for t, ref in enumerate((own_ref, *sent)):
        for h in range(own_ref.shape[0]):
            x = lax.rem(here_x + t, SX)
            y = lax.rem(here_y + h, own_ref.shape[0])
            start = pl.multiple_of((y * SX + x) * share, share)
            for g in range(gram_ref.shape[0]):
                ref[h, g * share : (g + 1) * share, :] = gram_ref[
                    g, pl.ds(start, share), :
                ].astype(ref.dtype)


def backward_kernel(devices, in_ref, table_ref, out_ref, rows_ref):
    comps = out_ref.shape[2]
    shots = out_ref.shape[4]
    size = out_ref.shape[5]
    rows_ref[...] = in_ref[...].astype(F32).reshape(rows_ref.shape)
    table = table_ref[...]
    for m in range(comps):
        res = dot(gathered(rows_ref, devices, comps, m), table, NN).astype(BF16)
        for d in range(2):
            for l in range(2):
                out_ref[0, d, m, l] = res[
                    l * shots : (l + 1) * shots, d * size : (d + 1) * size
                ]


def whole(shape):
    return pl.BlockSpec(shape, lambda *_: (0,) * len(shape))


def params():
    return pltpu.CompilerParams(dimension_semantics=("arbitrary",))


def per_device(data, mixing, counts):
    bins, _, comps, lines, shots, ry = data.shape
    rx = mixing.shape[5]
    devices = lax.axis_size("rx")
    shot_devices = lax.axis_size("shot")
    per = 2 * comps * 2
    lanes = lines * shots
    blocks = jax.ShapeDtypeStruct((devices, bins * per, lanes), BF16)
    block = pl.BlockSpec((devices, per, lanes), lambda f: (0, f, 0))
    rows = pltpu.VMEM((devices * per, lanes), F32)
    forward_y = dft_table(ry, 1.0)
    forward_x = dft_table(rx, 1.0)
    inverse_x = dft_table(rx, -1.0)
    inverse_y = dft_table(ry, -1.0)
    table = whole((2 * rx, 2 * rx))
    field = pl.BlockSpec((1,) + data.shape[1:], lambda f: (f, 0, 0, 0, 0, 0))

    sent = pl.pallas_call(
        functools.partial(forward_kernel, devices),
        grid=(bins,),
        out_shape=blocks,
        in_specs=[field, table],
        out_specs=block,
        scratch_shapes=[rows],
        compiler_params=params(),
        name="forward",
    )(data, out_rows(forward_y, 2))
    pencils = lax.all_to_all(sent, "rx", 0, 0, tiled=True)
    spaced, down = pl.pallas_call(
        functools.partial(middle_kernel, devices),
        grid=(bins,),
        out_shape=(blocks, jax.ShapeDtypeStruct((bins, lanes, 2 * rx), BF16)),
        in_specs=[
            pl.BlockSpec(memory_space=pltpu.SMEM),
            block,
            pl.BlockSpec((1,) + mixing.shape[1:], lambda f: (f, 0, 0, 0, 0, 0)),
            table,
            table,
        ],
        out_specs=(block, pl.BlockSpec((1, lanes, 2 * rx), lambda f: (f, 0, 0))),
        scratch_shapes=[rows, pltpu.VMEM((comps, lanes, 2 * rx), F32)],
        compiler_params=params(),
        name="middle",
    )(counts, pencils, mixing, in_rows(forward_x, 2), out_rows(inverse_x, 2))
    returned = lax.all_to_all(spaced, "rx", 0, 0, tiled=True)

    sy = shot_devices // SX
    share = rx // shot_devices
    here = lax.axis_index("shot")
    where = jnp.stack([here % SX, here // SX]).astype(jnp.int32)
    part = (sy, bins * 2 * 2 * share, rx)
    own, *parts = pl.pallas_call(
        functools.partial(gram_kernel, 1.0 / (shots * shot_devices)),
        out_shape=[jax.ShapeDtypeStruct(part, F32)]
        + [jax.ShapeDtypeStruct(part, BF16)] * (SX - 1),
        in_specs=[
            pl.BlockSpec(memory_space=pltpu.SMEM),
            pl.BlockSpec(memory_space=pltpu.VMEM),
            pl.BlockSpec(memory_space=pltpu.VMEM),
        ],
        out_specs=[pl.BlockSpec(memory_space=pltpu.VMEM)] * SX,
        scratch_shapes=[pltpu.VMEM((bins * 2 * 2, rx, rx), F32)],
        cost_estimate=pl.CostEstimate(flops=10**8, bytes_accessed=10**6, transcendentals=0),
        name="gram",
    )(where, down, bf16_const(inverse_x.transpose(2, 3, 0, 1).reshape(2 * rx, 2 * rx)))
    total = own
    for t in range(1, SX):
        pairs = [(s, s // SX * SX + (s % SX + t) % SX) for s in range(shot_devices)]
        total = total + lax.ppermute(parts[t - 1], "shot", pairs).astype(F32)
    gram = total[0]
    for h in range(1, sy):
        pairs = [(s, (s + h * SX) % shot_devices) for s in range(shot_devices)]
        gram = gram + lax.ppermute(total[h].astype(BF16), "shot", pairs).astype(F32)
    gram = gram.reshape(bins, 2, 2, share, rx)

    fields = pl.pallas_call(
        functools.partial(backward_kernel, devices),
        grid=(bins,),
        out_shape=jax.ShapeDtypeStruct(data.shape, BF16),
        in_specs=[block, table],
        out_specs=field,
        scratch_shapes=[rows],
        compiler_params=params(),
        name="backward",
    )(returned, in_rows(inverse_y, 2))
    return (fields, gram)


def solution(mesh):
    placed = (
        P(None, None, None, "rx", "shot", None),
        P(None, None, None, None, "rx", None),
        P(None, "rx"),
    )
    return jax.shard_map(
        per_device,
        mesh=mesh,
        in_specs=placed,
        out_specs=(P(None, None, None, "rx", "shot", None), P(None, None, "rx", "shot", None)),
        check_vma=False,
    )
```

```python
import functools
import math

import jax
import jax.numpy as jnp
import ml_dtypes
import numpy as np
from jax import lax
from jax.experimental import pallas as pl
from jax.experimental.pallas import tpu as pltpu
from jax.sharding import PartitionSpec as P


BF16 = jnp.bfloat16
F32 = jnp.float32
NT = (((1,), (1,)), ((), ()))
NN = (((1,), (0,)), ((), ()))
SX = 4
LIMIT = 16 * 2**20


def dft_table(size, sign):
    steps = np.arange(size, dtype=np.int64)
    angles = (steps[:, None] * steps[None, :] % size).astype(np.float64) * (2.0 * math.pi / size)
    cosine = np.cos(angles) / math.sqrt(size)
    sine = np.sin(angles) * (sign / math.sqrt(size))
    return np.stack(
        [np.stack([cosine, -sine], axis=1), np.stack([sine, cosine], axis=1)], axis=0
    )


def bf16_const(array):
    return np.ascontiguousarray(array).astype(np.float32).astype(ml_dtypes.bfloat16)


def out_rows(table, per):
    n = table.shape[1]
    t = table.reshape(2, n, 2, n // per, per)
    return bf16_const(t.transpose(2, 4, 3, 0, 1).reshape(2 * n, 2 * n))


def in_rows(table, per):
    n = table.shape[1]
    t = table.reshape(2, n // per, per, 2, n)
    return bf16_const(t.transpose(2, 0, 1, 3, 4).reshape(2 * n, 2 * n))


def dot(a, b, dims):
    return lax.dot_general(a, b, dims, preferred_element_type=F32)


def spread(rows_ref, devices, comps, f, m, res):
    step = rows_ref.shape[1] // devices
    for d in range(2):
        for p in range(2):
            start = (d * 2 + p) * devices
            rows_ref[f, pl.ds((d * comps + m) * 2 + p, devices, stride=step), :] = res[
                start : start + devices
            ]


def put(out_ref, block_ref, rows_ref, sems, f):
    devices, per = block_ref.shape[1:3]
    step = rows_ref.shape[1] // devices
    for j in range(devices):
        block_ref[f, j] = rows_ref[f, j * step : j * step + per, :].astype(BF16)
    copy = pltpu.make_async_copy(
        block_ref.at[f], out_ref.at[:, f * per : (f + 1) * per, :], sems.at[f]
    )
    copy.start()
    return copy


def take(rows_ref, in_ref, per, f):
    devices = in_ref.shape[0]
    step = rows_ref.shape[1] // devices
    for j in range(devices):
        rows_ref[f, j * step : j * step + per, :] = in_ref[j, f * per : (f + 1) * per, :].astype(F32)


def gathered(rows_ref, devices, comps, f, m):
    step = rows_ref.shape[1] // devices
    halves = []
    for p in range(2):
        both = jnp.concatenate(
            [rows_ref[f, pl.ds((c * comps + m) * 2 + p, devices, stride=step), :] for c in range(2)],
            axis=0,
        )
        turned = both.T.astype(BF16)
        half = turned.shape[0] // 2
        halves.append(jnp.concatenate([turned[:half], turned[half:]], axis=1))
    return jnp.concatenate(halves, axis=0)


def forward_kernel(
    devices, data_ref, table_ref, out_ref, in_ref, tab_ref, rows_ref, block_ref, sems, out_sems
):
    bins, _, comps = data_ref.shape[:3]
    lines = data_ref.shape[3] * data_ref.shape[4]
    size = data_ref.shape[5]
    loads = [
        pltpu.make_async_copy(data_ref.at[f], in_ref.at[f], sems.at[f]) for f in range(bins)
    ]
    load_table = pltpu.make_async_copy(table_ref, tab_ref, sems.at[bins])
    loads[0].start()
    load_table.start()
    for load in loads[1:]:
        load.start()
    load_table.wait()
    stores = []
    for f in range(bins):
        loads[f].wait()
        for m in range(comps):
            both = jnp.concatenate(
                [in_ref[f, c, m].reshape(lines, size) for c in range(2)], axis=1
            )
            spread(rows_ref, devices, comps, f, m, dot(tab_ref[...], both, NT))
        stores.append(put(out_ref, block_ref, rows_ref, out_sems, f))
    for store in stores:
        store.wait()


def middle_kernel(
    devices,
    counts_ref,
    in_ref,
    mixing_ref,
    fwd_ref,
    inv_ref,
    out_ref,
    down_ref,
    rows_ref,
    k_ref,
    block_ref,
    out_sems,
):
    bins, _, comps = mixing_ref.shape[:3]
    size = mixing_ref.shape[5]
    shots = in_ref.shape[2] // 2
    wave = lax.broadcasted_iota(jnp.int32, (1, size), 1)
    radial = jnp.minimum(wave, size - wave)
    stores = []
    for f in range(bins):
        take(rows_ref, in_ref, 2 * comps * 2, f)
        for m in range(comps):
            k_ref[f, m] = dot(gathered(rows_ref, devices, comps, f, m), fwd_ref[...], NN)
        for o in range(comps):
            parts = []
            for p in range(2):
                passing = (radial <= counts_ref[f, p]).astype(F32)
                span = pl.ds(p * shots, shots)
                real = imag = None
                for i in range(comps):
                    a = mixing_ref[f, 0, o, i, p : p + 1, :] * passing
                    b = mixing_ref[f, 1, o, i, p : p + 1, :] * passing
                    kr = k_ref[f, i, span, 0:size]
                    ki = k_ref[f, i, span, size : 2 * size]
                    r = a * kr - b * ki
                    s = a * ki + b * kr
                    real = r if real is None else real + r
                    imag = s if imag is None else imag + s
                parts.append(jnp.concatenate([real, imag], axis=1).astype(BF16))
            mixed = jnp.concatenate(parts, axis=0)
            if o == 1:
                down_ref[f] = mixed
            spread(rows_ref, devices, comps, f, o, dot(inv_ref[...], mixed, NT))
        stores.append(put(out_ref, block_ref, rows_ref, out_sems, f))
    for store in stores:
        store.wait()


def gram_kernel(weight, down_ref, inv_ref, own_ref, *rest):
    sent, gram_ref = rest[:-1], rest[-1]
    bins = down_ref.shape[0]
    size = down_ref.shape[2] // 2
    sy = own_ref.shape[0]
    share = size // (sy * SX)
    here = lax.axis_index("shot")
    here_x, here_y = lax.rem(here, SX), lax.div(here, SX)
    lane = lax.broadcasted_iota(jnp.int32, (1, down_ref.shape[1]), 1)
    shots = down_ref.shape[1] // 2
    for f in range(bins):
        spaced = dot(inv_ref[...], down_ref[f], NT).astype(BF16)
        real, imag = spaced[:size], spaced[size:]
        zero = jnp.zeros_like(real)
        left = jnp.concatenate([real, imag], axis=1)
        right = jnp.concatenate([left, jnp.concatenate([-imag, real], axis=1)], axis=0)
        for p in range(2):
            keep = (lane >= p * shots) & (lane < (p + 1) * shots)
            part = jnp.concatenate(
                [jnp.where(keep, real, zero), jnp.where(keep, imag, zero)], axis=1
            )
            prod = dot(part, right, NT) * weight
            for c in range(2):
                gram_ref[(f * 2 + c) * 2 + p] = prod[:, c * size : (c + 1) * size]
    for t, ref in enumerate((own_ref, *sent)):
        for h in range(sy):
            x = lax.rem(here_x + t, SX)
            y = lax.rem(here_y + h, sy)
            start = pl.multiple_of((y * SX + x) * share, share)
            for g in range(gram_ref.shape[0]):
                ref[h, g * share : (g + 1) * share, :] = gram_ref[
                    g, pl.ds(start, share), :
                ].astype(ref.dtype)


def backward_kernel(devices, in_ref, table_ref, out_ref, rows_ref, res_ref, sems):
    bins, _, comps, lines, shots, size = out_ref.shape
    stores = []
    for f in range(bins):
        take(rows_ref, in_ref, 2 * comps * 2, f)
        for m in range(comps):
            res = dot(gathered(rows_ref, devices, comps, f, m), table_ref[...], NN).astype(BF16)
            for d in range(2):
                for l in range(lines):
                    res_ref[f, d, m, l] = res[
                        l * shots : (l + 1) * shots, d * size : (d + 1) * size
                    ]
            store = pltpu.make_async_copy(
                res_ref.at[f, :, m], out_ref.at[f, :, m], sems.at[f * comps + m]
            )
            store.start()
            stores.append(store)
    for store in stores:
        store.wait()


def params():
    return pltpu.CompilerParams(vmem_limit_bytes=LIMIT)


def per_device(data, mixing, counts):
    bins, _, comps, lines, shots, ry = data.shape
    rx = mixing.shape[5]
    devices = lax.axis_size("rx")
    shot_devices = lax.axis_size("shot")
    per = 2 * comps * 2
    lanes = lines * shots
    blocks = jax.ShapeDtypeStruct((devices, bins * per, lanes), BF16)
    rows = pltpu.VMEM((bins, devices * (per + 1), lanes), F32)
    block = pltpu.VMEM((bins, devices, per, lanes), BF16)
    forward_y = dft_table(ry, 1.0)
    forward_x = dft_table(rx, 1.0)
    inverse_x = dft_table(rx, -1.0)
    inverse_y = dft_table(ry, -1.0)
    vmem = pl.BlockSpec(memory_space=pltpu.VMEM)
    outside = pl.BlockSpec(memory_space=pl.ANY)
    fields_shape = jax.ShapeDtypeStruct(data.shape, BF16)

    sent = pl.pallas_call(
        functools.partial(forward_kernel, devices),
        out_shape=blocks,
        in_specs=[outside, outside],
        out_specs=outside,
        scratch_shapes=[
            pltpu.VMEM(data.shape, BF16),
            pltpu.VMEM((2 * ry, 2 * ry), BF16),
            rows,
            block,
            pltpu.SemaphoreType.DMA((bins + 1,)),
            pltpu.SemaphoreType.DMA((bins,)),
        ],
        name="forward",
    )(data, out_rows(forward_y, 2))
    pencils = lax.all_to_all(sent, "rx", 0, 0, tiled=True)
    spaced, down = pl.pallas_call(
        functools.partial(middle_kernel, devices),
        out_shape=(blocks, jax.ShapeDtypeStruct((bins, lanes, 2 * rx), BF16)),
        in_specs=[pl.BlockSpec(memory_space=pltpu.SMEM), vmem, vmem, vmem, vmem],
        out_specs=(outside, vmem),
        scratch_shapes=[
            rows,
            pltpu.VMEM((bins, comps, lanes, 2 * rx), F32),
            block,
            pltpu.SemaphoreType.DMA((bins,)),
        ],
        compiler_params=params(),
        name="middle",
    )(counts, pencils, mixing, in_rows(forward_x, 2), out_rows(inverse_x, 2))
    returned = lax.all_to_all(spaced, "rx", 0, 0, tiled=True)

    sy = shot_devices // SX
    share = rx // shot_devices
    part = (sy, bins * 2 * 2 * share, rx)
    own, *parts = pl.pallas_call(
        functools.partial(gram_kernel, 1.0 / (shots * shot_devices)),
        out_shape=[jax.ShapeDtypeStruct(part, F32)]
        + [jax.ShapeDtypeStruct(part, BF16)] * (SX - 1),
        in_specs=[vmem, vmem],
        out_specs=[vmem] * SX,
        scratch_shapes=[pltpu.VMEM((bins * 2 * 2, rx, rx), F32)],
        compiler_params=params(),
        cost_estimate=pl.CostEstimate(flops=10**8, bytes_accessed=10**6, transcendentals=0),
        name="gram",
    )(down, bf16_const(inverse_x.transpose(2, 3, 0, 1).reshape(2 * rx, 2 * rx)))
    total = own
    for t in range(1, SX):
        pairs = [(s, s // SX * SX + (s % SX + t) % SX) for s in range(shot_devices)]
        total = total + lax.ppermute(parts[t - 1], "shot", pairs).astype(F32)
    gram = total[0]
    for h in range(1, sy):
        pairs = [(s, (s + h * SX) % shot_devices) for s in range(shot_devices)]
        far = lax.ppermute(total[h].astype(BF16), "shot", pairs)
        gram = gram + far.astype(F32)
    gram = gram.reshape(bins, 2, 2, share, rx)

    fields_of = pl.pallas_call(
        functools.partial(backward_kernel, devices),
        out_shape=fields_shape,
        in_specs=[vmem, vmem],
        out_specs=outside,
        scratch_shapes=[rows, pltpu.VMEM(data.shape, BF16), pltpu.SemaphoreType.DMA((bins * comps,))],
        compiler_params=params(),
        name="backward",
    )
    fields = fields_of(returned, in_rows(inverse_y, 2))
    return (fields, gram)


def solution(mesh):
    placed = (
        P(None, None, None, "rx", "shot", None),
        P(None, None, None, None, "rx", None),
        P(None, "rx"),
    )

    return jax.shard_map(
        per_device,
        mesh=mesh,
        in_specs=placed,
        out_specs=(P(None, None, None, "rx", "shot", None), P(None, None, "rx", "shot", None)),
        check_vma=False,
    )
```

```python
import functools
import math

import jax
import jax.numpy as jnp
import ml_dtypes
import numpy as np
from jax import lax
from jax.experimental import pallas as pl
from jax.experimental.pallas import tpu as pltpu
from jax.sharding import PartitionSpec as P


BF16 = jnp.bfloat16
F32 = jnp.float32
NT = (((1,), (1,)), ((), ()))
NN = (((1,), (0,)), ((), ()))
SX = 4
CHUNK = 8
LIMIT = 16 * 2**20
ORDER = [
    37, 0, 27, 13, 19, 54, 55, 40, 17, 53, 43, 14, 28, 23, 51, 9,
    52, 62, 44, 50, 25, 10, 63, 6, 20, 16, 61, 32, 56, 45, 7, 36,
    3, 30, 60, 33, 24, 11, 47, 4, 34, 59, 46, 22, 1, 26, 35, 8,
    21, 38, 15, 29, 18, 49, 58, 41, 5, 39, 12, 31, 57, 48, 42, 2,
]


def dft_table(size, sign):
    steps = np.arange(size, dtype=np.int64)
    angles = (steps[:, None] * steps[None, :] % size).astype(np.float64) * (2.0 * math.pi / size)
    cosine = np.cos(angles) / math.sqrt(size)
    sine = np.sin(angles) * (sign / math.sqrt(size))
    return np.stack(
        [np.stack([cosine, -sine], axis=1), np.stack([sine, cosine], axis=1)], axis=0
    )


def bf16_const(array):
    return np.ascontiguousarray(array).astype(np.float32).astype(ml_dtypes.bfloat16)


def out_rows(table, per):
    n = table.shape[1]
    t = table.reshape(2, n, 2, n // per, per)[:, :, :, ORDER]
    return bf16_const(t.transpose(2, 4, 3, 0, 1).reshape(2 * n, 2 * n))


def in_rows(table, per):
    n = table.shape[1]
    t = table.reshape(2, n // per, per, 2, n)[:, ORDER]
    return bf16_const(t.transpose(2, 0, 1, 3, 4).reshape(2 * n, 2 * n))


def dot(a, b, dims):
    return lax.dot_general(a, b, dims, preferred_element_type=F32)


def spread(rows_ref, devices, comps, f, m, res):
    step = rows_ref.shape[1] // devices
    for d in range(2):
        for p in range(2):
            start = (d * 2 + p) * devices
            rows_ref[f, pl.ds((d * comps + m) * 2 + p, devices, stride=step), :] = res[
                start : start + devices
            ]


def put(out_ref, block_ref, rows_ref, sems, f):
    devices, per = block_ref.shape[1:3]
    step = rows_ref.shape[1] // devices
    for j in range(devices):
        block_ref[f, j] = rows_ref[f, j * step : j * step + per, :].astype(BF16)
    copy = pltpu.make_async_copy(
        block_ref.at[f], out_ref.at[:, f * per : (f + 1) * per, :], sems.at[f]
    )
    copy.start()
    return copy


def take(rows_ref, in_ref, per, f):
    devices = in_ref.shape[0]
    step = rows_ref.shape[1] // devices
    for j in range(devices):
        rows_ref[f, j * step : j * step + per, :] = in_ref[j, f * per : (f + 1) * per, :].astype(F32)


def gathered(rows_ref, devices, comps, f, m):
    step = rows_ref.shape[1] // devices
    halves = []
    for p in range(2):
        both = jnp.concatenate(
            [rows_ref[f, pl.ds((c * comps + m) * 2 + p, devices, stride=step), :] for c in range(2)],
            axis=0,
        )
        turned = both.astype(BF16).T
        half = turned.shape[0] // 2
        halves.append(jnp.concatenate([turned[:half], turned[half:]], axis=1))
    return jnp.concatenate(halves, axis=0)


def forward_kernel(
    devices, data_ref, table_ref, out_ref, in_ref, tab_ref, rows_ref, block_ref, sems, out_sems
):
    bins, _, comps = data_ref.shape[:3]
    lines = data_ref.shape[3] * data_ref.shape[4]
    size = data_ref.shape[5]
    loads = [
        pltpu.make_async_copy(data_ref.at[f], in_ref.at[f], sems.at[f]) for f in range(bins)
    ]
    load_table = pltpu.make_async_copy(table_ref, tab_ref, sems.at[bins])
    loads[0].start()
    load_table.start()
    for load in loads[1:]:
        load.start()
    load_table.wait()
    stores = []
    for f in range(bins):
        loads[f].wait()
        for m in range(comps):
            both = jnp.concatenate(
                [in_ref[f, c, m].reshape(lines, size) for c in range(2)], axis=1
            )
            spread(rows_ref, devices, comps, f, m, dot(tab_ref[...], both, NT))
        stores.append(put(out_ref, block_ref, rows_ref, out_sems, f))
    for store in stores:
        store.wait()


def coefs_kernel(counts_ref, mixing_ref, out_ref):
    size = mixing_ref.shape[5]
    wave = lax.broadcasted_iota(jnp.int32, (2, size), 1)
    place = lax.broadcasted_iota(jnp.int32, (2, size), 0)
    radial = jnp.minimum(wave, size - wave)
    for f in range(mixing_ref.shape[0]):
        passing = radial <= jnp.where(place == 0, counts_ref[f, 0], counts_ref[f, 1])
        for o in range(mixing_ref.shape[2]):
            for i in range(mixing_ref.shape[3]):
                a = jnp.where(passing, mixing_ref[f, 0, o, i], 0.0)
                b = jnp.where(passing, mixing_ref[f, 1, o, i], 0.0)
                out_ref[f, 0, o, i] = a
                out_ref[f, 1, o, i] = a + b
                out_ref[f, 2, o, i] = b - a


def middle_kernel(
    devices, in_ref, coefs_ref, fwd_ref, inv_ref, out_ref, down_ref, rows_ref, k_ref, mixed_ref,
    block_ref, out_sems,
):
    bins, _, comps = coefs_ref.shape[:3]
    size = coefs_ref.shape[5]
    shots = in_ref.shape[2] // 2

    def transformed(f, m):
        k = dot(gathered(rows_ref, devices, comps, f, m), fwd_ref[...], NN)
        k_ref[f, m, :, 0 : 2 * size] = k
        k_ref[f, m, :, 2 * size : 3 * size] = k[:, :size] + k[:, size:]

    def mixed(f, o):
        into = down_ref.at[f] if o == 1 else mixed_ref.at[f, o]
        for p in range(2):
            for start in range(p * shots, (p + 1) * shots, CHUNK):
                span = slice(start, start + CHUNK)
                both = real = imag = None
                for i in range(comps):
                    a, u, v = (coefs_ref[f, c, o, i, p : p + 1, :] for c in range(3))
                    q = a * k_ref[f, i, span, 2 * size : 3 * size]
                    r = u * k_ref[f, i, span, size : 2 * size]
                    s = v * k_ref[f, i, span, 0:size]
                    both = q if both is None else both + q
                    real = r if real is None else real + r
                    imag = s if imag is None else imag + s
                into[span, 0:size] = (both - real).astype(BF16)
                into[span, size : 2 * size] = (both + imag).astype(BF16)

    def back(f, o):
        into = down_ref.at[f] if o == 1 else mixed_ref.at[f, o]
        spread(rows_ref, devices, comps, f, o, dot(inv_ref[...], into[...], NT))

    stores = []
    take(rows_ref, in_ref, 2 * comps * 2, 0)
    for m in range(comps):
        transformed(0, m)
    for f in range(bins):
        if f + 1 < bins:
            take(rows_ref, in_ref, 2 * comps * 2, f + 1)
        for o in range(comps):
            if f + 1 < bins:
                transformed(f + 1, o)
            mixed(f, o)
            if o > 0:
                back(f, o - 1)
        back(f, comps - 1)
        stores.append(put(out_ref, block_ref, rows_ref, out_sems, f))
    for store in stores:
        store.wait()


def gram_kernel(weight, down_ref, inv_ref, *rest):
    *sent, lines_ref = rest
    bins, lanes = down_ref.shape[:2]
    size = down_ref.shape[2] // 2
    sy = sent[0].shape[0]
    share = size // (sy * SX)
    here = lax.axis_index("shot")
    here_x, here_y = lax.rem(here, SX), lax.div(here, SX)
    lane = lax.broadcasted_iota(jnp.int32, (1, lanes), 1)
    keep = [(lane >= p * lanes // 2) & (lane < (p + 1) * lanes // 2) for p in range(2)]
    starts = []
    for t in range(SX):
        for h in range(sy):
            x, y = lax.rem(here_x + t, SX), lax.rem(here_y + h, sy)
            starts.append(pl.multiple_of((y * SX + x) * share, share))
    for f in range(bins):
        lines_ref[f] = dot(inv_ref[...], down_ref[f], NT).astype(BF16)
    prods = []
    for f in range(bins):
        real, imag = lines_ref[f, :size], lines_ref[f, size:]
        right = jnp.concatenate(
            [jnp.concatenate([real, imag], axis=1), jnp.concatenate([-imag, real], axis=1)],
            axis=0,
        )
        parts = [
            jnp.concatenate(
                [lines_ref[f, pl.ds(c * size + start, share), :] for start in starts], axis=0
            )
            for c in range(2)
        ]
        left = [
            jnp.concatenate([jnp.where(k, q, jnp.zeros_like(q)) for q in parts], axis=1)
            for k in keep
        ]
        prods.append(dot(jnp.concatenate(left, axis=0), right, NT))
    for f in range(bins):
        for p in range(2):
            for n in range(len(starts)):
                ref = sent[n // sy]
                row = p * size + n * share
                for c in range(2):
                    g = (f * 2 + c) * 2 + p
                    ref[n % sy, g * share : (g + 1) * share, :] = (
                        prods[f][row : row + share, c * size : (c + 1) * size] * weight
                    ).astype(ref.dtype)


def backward_kernel(devices, in_ref, table_ref, out_ref, rows_ref, res_ref, sems):
    bins, _, comps, lines, shots, size = out_ref.shape
    stores = []
    for f in range(bins):
        take(rows_ref, in_ref, 2 * comps * 2, f)
        for m in range(comps):
            res = dot(gathered(rows_ref, devices, comps, f, m), table_ref[...], NN).astype(BF16)
            for d in range(2):
                for l in range(lines):
                    res_ref[f, d, m, l] = res[
                        l * shots : (l + 1) * shots, d * size : (d + 1) * size
                    ]
        store = pltpu.make_async_copy(res_ref.at[f], out_ref.at[f], sems.at[f])
        store.start()
        stores.append(store)
    for store in stores:
        store.wait()


def exchange(blocks):
    return lax.all_to_all(blocks, "rx", 0, 0, tiled=True, axis_index_groups=[ORDER])


def params():
    return pltpu.CompilerParams(vmem_limit_bytes=LIMIT)


def per_device(data, mixing, counts):
    bins, _, comps, lines, shots, ry = data.shape
    rx = mixing.shape[5]
    devices = lax.axis_size("rx")
    shot_devices = lax.axis_size("shot")
    per = 2 * comps * 2
    lanes = lines * shots
    blocks = jax.ShapeDtypeStruct((devices, bins * per, lanes), BF16)
    rows = pltpu.VMEM((bins, devices * (per + 1), lanes), F32)
    block = pltpu.VMEM((bins, devices, per, lanes), BF16)
    forward_y = dft_table(ry, 1.0)
    forward_x = dft_table(rx, 1.0)
    inverse_x = dft_table(rx, -1.0)
    inverse_y = dft_table(ry, -1.0)
    vmem = pl.BlockSpec(memory_space=pltpu.VMEM)
    outside = pl.BlockSpec(memory_space=pl.ANY)
    fields_shape = jax.ShapeDtypeStruct(data.shape, BF16)

    sent = pl.pallas_call(
        functools.partial(forward_kernel, devices),
        out_shape=blocks,
        in_specs=[outside, outside],
        out_specs=outside,
        scratch_shapes=[
            pltpu.VMEM(data.shape, BF16),
            pltpu.VMEM((2 * ry, 2 * ry), BF16),
            rows,
            block,
            pltpu.SemaphoreType.DMA((bins + 1,)),
            pltpu.SemaphoreType.DMA((bins,)),
        ],
        name="forward",
    )(data, out_rows(forward_y, 2))
    pencils = exchange(sent)
    coefs = pl.pallas_call(
        coefs_kernel,
        out_shape=jax.ShapeDtypeStruct((bins, 3, comps, comps, 2, rx), F32),
        in_specs=[pl.BlockSpec(memory_space=pltpu.SMEM), vmem],
        out_specs=vmem,
        compiler_params=params(),
        cost_estimate=pl.CostEstimate(flops=10**6, bytes_accessed=10**6, transcendentals=0),
        name="coefs",
    )(counts, mixing)
    spaced, down = pl.pallas_call(
        functools.partial(middle_kernel, devices),
        out_shape=(blocks, jax.ShapeDtypeStruct((bins, lanes, 2 * rx), BF16)),
        in_specs=[vmem, vmem, vmem, vmem],
        out_specs=(outside, vmem),
        scratch_shapes=[
            rows,
            pltpu.VMEM((bins, comps, lanes, 3 * rx), F32),
            pltpu.VMEM((bins, comps, lanes, 2 * rx), BF16),
            block,
            pltpu.SemaphoreType.DMA((bins,)),
        ],
        compiler_params=params(),
        name="middle",
    )(pencils, coefs, in_rows(forward_x, 2), out_rows(inverse_x, 2))
    returned = exchange(spaced)

    sy = shot_devices // SX
    share = rx // shot_devices
    part = (sy, bins * 2 * 2 * share, rx)
    own, *parts = pl.pallas_call(
        functools.partial(gram_kernel, 1.0 / (shots * shot_devices)),
        out_shape=[jax.ShapeDtypeStruct(part, F32)]
        + [jax.ShapeDtypeStruct(part, BF16)] * (SX - 1),
        in_specs=[vmem, vmem],
        out_specs=[vmem] * SX,
        scratch_shapes=[pltpu.VMEM((bins, 2 * rx, lanes), BF16)],
        compiler_params=params(),
        cost_estimate=pl.CostEstimate(flops=10**8, bytes_accessed=10**6, transcendentals=0),
        name="gram",
    )(down, bf16_const(inverse_x.transpose(2, 3, 0, 1).reshape(2 * rx, 2 * rx)))
    total = own
    for t in range(1, SX):
        pairs = [(s, s // SX * SX + (s % SX + t) % SX) for s in range(shot_devices)]
        total = total + lax.ppermute(parts[t - 1], "shot", pairs).astype(F32)
    gram = total[0]
    for h in range(1, sy):
        pairs = [(s, (s + h * SX) % shot_devices) for s in range(shot_devices)]
        far = lax.ppermute(total[h].astype(BF16), "shot", pairs)
        gram = gram + far.astype(F32)
    gram = gram.reshape(bins, 2, 2, share, rx)

    fields_of = pl.pallas_call(
        functools.partial(backward_kernel, devices),
        out_shape=fields_shape,
        in_specs=[vmem, vmem],
        out_specs=outside,
        scratch_shapes=[rows, pltpu.VMEM(data.shape, BF16), pltpu.SemaphoreType.DMA((bins,))],
        compiler_params=params(),
        name="backward",
    )
    fields = fields_of(returned, in_rows(inverse_y, 2))
    return (fields, gram)


def solution(mesh):
    placed = (
        P(None, None, None, "rx", "shot", None),
        P(None, None, None, None, "rx", None),
        P(None, "rx"),
    )

    return jax.shard_map(
        per_device,
        mesh=mesh,
        in_specs=placed,
        out_specs=(P(None, None, None, "rx", "shot", None), P(None, None, "rx", "shot", None)),
        check_vma=False,
    )
```
